128 devices in a mesh: dp: 16 (over y, x_hi, core), mp: 8 (over x_lo, z).
Axes of the slice: x: 4 (x_hi: 2, x_lo: 2; x = x_hi * 2 + x_lo), y: 4, z: 4, core: 2. Of those that a mesh axis runs over, the one named last changes fastest.
Arguments:
- inputs: bfloat16 [16384, 3072], P(('dp', 'mp')), may hold values from -64 to 64, as said below
- w_qkv: bfloat16 [3072, 3, 3072], P('dp', None, 'mp'), may hold values from -2 to 2
- w_out: bfloat16 [3072, 3072], P('mp', 'dp'), may hold values from -0.109375 to 0.109375
- upstream: bfloat16 [16384, 3072], P(('dp', 'mp')), may hold values from -6 to 6
Outputs:
- layer_out: bfloat16 [16384, 3072], P(('dp', 'mp'))
- grad_x: bfloat16 [16384, 3072], P(('dp', 'mp'))
- grad_wqkv: bfloat16 [3072, 3, 3072], P('dp', None, 'mp')
- grad_wout: bfloat16 [3072, 3072], P('mp', 'dp')
The draws below stay inside these ranges and needn't reach their ends.
Inputs may be any that keep to these rules, and one draw needn't show every extreme that they name: `inputs`: Activations; each row's scale may differ.
All inputs are finite; a program needn't handle non-finite values.
Results may differ from the reference program's by a relative error of at most 0.014.
The reference program's roundings to bfloat16 on the way (of `normed`, `projected`, `probs16`, `context`, `grad_context`, `grad_values`, `grad_scores` and `grad_projected`) count: a program that leaves them out, or rounds other values in their place, can miss the bound.
Values may be sent and summed in bfloat16 or wider, within the bound.
No kernel may reach another device: no remote copies, remote signals or barrier semaphores. Data moves between devices by JAX's collectives and lax.ppermute only.
A program may use at most 128 MiB of HBM per device.

```python
import jax
import jax.numpy as jnp
from jax import lax

D = 3072
HEADS = 24
HD = 128
PATCH = 256
IMG_DEV = 4
A = 3072
TOKENS = 16384
N_DP = 16
N_MP = 8


def draw_inputs(key, part):
    first_key = jax.random.fold_in(key, 0)
    base = jnp.clip(jax.random.normal(first_key, (TOKENS, D), jnp.float32), -6.0, 6.0)
    return base.astype(jnp.bfloat16)


def draw_w_qkv(key, part):
    query_key, key_key, value_key = jax.random.split(key, 3)
    spread = D ** (-0.5)
    queries = jnp.clip(jax.random.normal(query_key, (D, 1, HEADS, HD), jnp.float32), -4.0, 4.0) * spread
    keys_part = jnp.clip(jax.random.normal(key_key, (D, 1, HEADS, HD), jnp.float32), -4.0, 4.0) * spread
    values_part = jnp.clip(jax.random.normal(value_key, (D, 1, HEADS, HD), jnp.float32), -4.0, 4.0) * spread
    return jnp.concatenate([queries, keys_part, values_part], axis=1).reshape(D, 3, HEADS * HD).astype(jnp.bfloat16)


def level_of(stream_key, shape, shards, smallest, largest):
    loudness, own = 1.0, jax.random.fold_in(stream_key, 6)
    for dim, parts in shards:
        steps = jnp.exp(jax.random.uniform(jax.random.fold_in(own, dim), (parts,), jnp.float32, smallest / len(shards), largest / len(shards)))
        loudness = loudness * jnp.repeat(steps, shape[dim] // parts).reshape([-1 if axis == dim else 1 for axis in range(len(shape))])
    return loudness


def scatter_about(own_key, extent, deviation, bound, cuts=(), dtype=jnp.bfloat16):
    gain = level_of(own_key, extent, cuts, -0.22, 0.18) if cuts else 1.0
    drawn = jax.random.normal(own_key, extent, jnp.float32) * deviation * gain
    return jnp.minimum(jnp.maximum(drawn, -bound), bound).astype(dtype)


def setup_inputs(seed: int = 0) -> dict:
    streams_of = jax.random.split(jax.random.key(seed), 5)
    inputs = draw_inputs(jax.random.fold_in(streams_of[4], 71), 0)
    w_qkv = draw_w_qkv(jax.random.fold_in(streams_of[4], 71), 0)
    w_out = scatter_about(streams_of[2], (A, D), A ** -0.5, 0.109375, ((0, 8), (1, 16)))
    upstream = scatter_about(streams_of[3], (TOKENS, D), 1.0, 6.0, ((0, 128),))
    return {"inputs": inputs, "w_qkv": w_qkv, "w_out": w_out, "upstream": upstream}


def rounded(values):
    return lax.optimization_barrier(values.astype(jnp.bfloat16)).astype(jnp.float32)

def reference(inputs, w_qkv, w_out, upstream):
    rows_group = IMG_DEV * PATCH
    local_width = A // N_MP
    inputs_float = inputs.astype(jnp.float32)
    centred = inputs_float - lax.optimization_barrier(jnp.mean(inputs_float, axis=1, keepdims=True))
    inv_scale = lax.rsqrt(lax.optimization_barrier(jnp.mean(centred * centred, axis=1, keepdims=True)) + 1e-06)
    standard = centred * inv_scale
    normed = standard.astype(jnp.bfloat16)
    projected = jnp.dot(normed, w_qkv.reshape(D, 3 * A), preferred_element_type=jnp.float32).astype(jnp.bfloat16)
    split_view = projected.reshape(TOKENS // PATCH, PATCH, 3, HEADS, HD)
    queries = split_view[:, :, 0].astype(jnp.float32)
    keys_part = split_view[:, :, 1].astype(jnp.float32)
    values_part = split_view[:, :, 2].astype(jnp.float32)
    scale = HD ** (-0.5)
    scores = jnp.einsum('bqhe,bkhe->bhqk', queries, keys_part) * scale
    probs = jax.nn.softmax(scores, axis=-1)
    probs16 = probs.astype(jnp.bfloat16)
    context = jnp.einsum('bhqk,bkhe->bqhe', probs16.astype(jnp.float32), values_part).astype(jnp.bfloat16).reshape(TOKENS, A)
    attended = jnp.zeros((TOKENS, D), jnp.float32)
    for shard in range(N_MP):
        low = shard * local_width
        attended = attended + rounded(jnp.dot(context[:, low:low + local_width], w_out[low:low + local_width], preferred_element_type=jnp.float32))
    layer_out = (inputs_float + attended).astype(jnp.bfloat16)
    grad_context = jnp.dot(upstream, w_out.T, preferred_element_type=jnp.float32).astype(jnp.bfloat16)
    grad_wout = jnp.zeros((A, D), jnp.float32)
    for group in range(N_DP):
        low = group * rows_group
        grad_wout = grad_wout + rounded(jnp.dot(context[low:low + rows_group].T, upstream[low:low + rows_group], preferred_element_type=jnp.float32))
    grad_heads = grad_context.reshape(TOKENS // PATCH, PATCH, HEADS, HD).astype(jnp.float32)
    grad_probs = jnp.einsum('bqhe,bkhe->bhqk', grad_heads, values_part)
    grad_values = jnp.einsum('bhqk,bqhe->bkhe', probs16.astype(jnp.float32), grad_heads).astype(jnp.bfloat16)
    row_totals = lax.optimization_barrier(jnp.sum(probs * grad_probs, axis=-1, keepdims=True))
    grad_scores = (probs * (grad_probs - row_totals) * scale).astype(jnp.bfloat16).astype(jnp.float32)
    grad_queries = jnp.einsum('bhqk,bkhe->bqhe', grad_scores, keys_part).astype(jnp.bfloat16)
    grad_keys = jnp.einsum('bhqk,bqhe->bkhe', grad_scores, queries).astype(jnp.bfloat16)
    grad_projected = jnp.stack([grad_queries, grad_keys, grad_values], axis=2).reshape(TOKENS, 3, A)
    grad_normed = jnp.zeros((TOKENS, D), jnp.float32)
    for shard in range(N_MP):
        low = shard * local_width
        piece = grad_projected[:, :, low:low + local_width].reshape(TOKENS, 3 * local_width)
        weight_piece = w_qkv[:, :, low:low + local_width].reshape(D, 3 * local_width)
        grad_normed = grad_normed + rounded(jnp.dot(piece, weight_piece.T, preferred_element_type=jnp.float32))
    centre_grad = lax.optimization_barrier(jnp.mean(grad_normed, axis=1, keepdims=True))
    along = lax.optimization_barrier(jnp.mean(grad_normed * standard, axis=1, keepdims=True))
    grad_x = (upstream.astype(jnp.float32) + inv_scale * (grad_normed - centre_grad - standard * along)).astype(jnp.bfloat16)
    flat_grad = grad_projected.reshape(TOKENS, 3 * A)
    grad_wqkv = jnp.zeros((D, 3 * A), jnp.float32)
    for group in range(N_DP):
        low = group * rows_group
        grad_wqkv = grad_wqkv + rounded(jnp.dot(normed[low:low + rows_group].T, flat_grad[low:low + rows_group], preferred_element_type=jnp.float32))
    grad_wqkv = grad_wqkv.reshape(D, 3, A).astype(jnp.bfloat16)
    return (layer_out, grad_x, grad_wqkv, grad_wout.astype(jnp.bfloat16))
```

```python
import functools

import jax
import jax.numpy as jnp
from jax import lax
from jax.experimental import pallas as pl
from jax.experimental.pallas import tpu as pltpu
from jax.sharding import Mesh, PartitionSpec as P

HD = 128
PATCH = 256
EPS = 1e-06
F32 = jnp.float32
BF16 = jnp.bfloat16
XY = ("y", "xh", "xl")
ALL = ("y", "xh", "c", "xl", "z")


def params(**kw):
    return pltpu.CompilerParams(vmem_limit_bytes=56 * 1024 * 1024, **kw)


def cost(flops, nbytes):
    return pl.CostEstimate(flops=int(flops), bytes_accessed=int(nbytes), transcendentals=0)


def hop(value, distance):
    return lax.ppermute(value, "z", [(i, i ^ distance) for i in range(4)])


def swap(value):
    return lax.ppermute(value, "c", [(0, 1), (1, 0)])


def halves(rows, core):
    count, width = rows.shape
    view = rows.reshape(count, 8, 2, width // 16)
    even = view[:, :, 0].reshape(count, width // 2)
    odd = view[:, :, 1].reshape(count, width // 2)
    first = jnp.where(core == 0, even, odd)
    second = jnp.where(core == 0, odd, even)
    return jnp.stack([first, second])


def whole(pair, core):
    _, count, half = pair.shape
    even = jnp.where(core == 0, pair[0], pair[1]).reshape(count, 8, 1, half // 8)
    odd = jnp.where(core == 0, pair[1], pair[0]).reshape(count, 8, 1, half // 8)
    return jnp.concatenate([even, odd], axis=2).reshape(count, 2 * half)


def both(ref):
    g, _, _, r, e = ref.shape
    return jnp.concatenate([ref[:, 0, 0].reshape(g * r, e), ref[:, 1, 0].reshape(g * r, e)], axis=1)


def project_kernel(x_ref, own_ref, other_ref, out_ref):
    total = jnp.dot(x_ref[0], both(own_ref), preferred_element_type=F32)
    total += jnp.dot(x_ref[1], both(other_ref), preferred_element_type=F32)
    out_ref[0] = total.astype(BF16)


def project(x, own, other):
    _, rows, half = x.shape
    g, _, planes, r, e = own.shape
    spec = pl.BlockSpec((g, 2, 1, r, e), lambda p: (0, 0, p, 0, 0))
    return pl.pallas_call(
        project_kernel,
        out_shape=jax.ShapeDtypeStruct((planes, rows, 2 * e), BF16),
        grid=(planes,),
        in_specs=[pl.BlockSpec((2, rows, half), lambda p: (0, 0, 0)), spec, spec],
        out_specs=pl.BlockSpec((1, rows, 2 * e), lambda p: (p, 0, 0)),
        compiler_params=params(),
        cost_estimate=cost(8 * rows * half * e * planes, 2 * (2 * x.size // 2 + own.size * 2)),
    )(x, own, other)


def attention_kernel(p_ref, g_ref, ctx_ref, d_ref):
    heads = g_ref.shape[1] // HD
    nt = (((1,), (1,)), ((), ()))
    tn = (((0,), (0,)), ((), ()))
    scale = HD ** (-0.5)
    for h in range(heads):
        cols = slice(h * HD, (h + 1) * HD)
        q, k, v, g = p_ref[0, :, cols], p_ref[1, :, cols], p_ref[2, :, cols], g_ref[:, cols]
        scores = lax.dot_general(q, k, nt, preferred_element_type=F32) * scale
        top = jnp.max(scores, axis=1, keepdims=True)
        weights = jnp.exp(scores - top)
        probs = weights / jnp.sum(weights, axis=1, keepdims=True)
        probs16 = probs.astype(BF16)
        ctx_ref[:, cols] = jnp.dot(probs16, v, preferred_element_type=F32).astype(BF16)
        gp = lax.dot_general(g, v, nt, preferred_element_type=F32)
        d_ref[2, :, cols] = lax.dot_general(probs16, g, tn, preferred_element_type=F32).astype(BF16)
        totals = jnp.sum(probs * gp, axis=1, keepdims=True)
        gs = (probs * (gp - totals) * scale).astype(BF16)
        d_ref[0, :, cols] = jnp.dot(gs, k, preferred_element_type=F32).astype(BF16)
        d_ref[1, :, cols] = lax.dot_general(gs, q, tn, preferred_element_type=F32).astype(BF16)


def attention(projected, grad_context):
    _, rows, width = projected.shape
    cols = 3 * HD
    three = pl.BlockSpec((3, PATCH, cols), lambda i, h: (0, i, h))
    one = pl.BlockSpec((PATCH, cols), lambda i, h: (i, h))
    return pl.pallas_call(
        attention_kernel,
        out_shape=[
            jax.ShapeDtypeStruct((rows, width), BF16),
            jax.ShapeDtypeStruct((3, rows, width), BF16),
        ],
        grid=(rows // PATCH, width // cols),
        in_specs=[three, one],
        out_specs=[one, three],
        compiler_params=params(),
        cost_estimate=cost(14 * rows * PATCH * width * 3, 2 * 8 * rows * width),
    )(projected, grad_context)


def back_kernel(d_ref, own_ref, other_ref, y0, y1, y2a, y2b, y3):
    nt = (((1,), (1,)), ((), ()))
    planes = own_ref.shape[2]
    outs = [(y0, y1, y2a, y3), (y0, y1, y2b, y3)]
    for half, ref in enumerate((own_ref, other_ref)):
        total = None
        for p in range(planes):
            g, _, _, r, e = ref.shape
            w = jnp.concatenate([ref[:, 0, p].reshape(g * r, e), ref[:, 1, p].reshape(g * r, e)], axis=1)
            term = lax.dot_general(d_ref[p], w, nt, preferred_element_type=F32)
            total = term if total is None else total + term
        total = total.astype(BF16)
        for j, out in enumerate(outs[half]):
            block = total[j * 128 : (j + 1) * 128]
            if j == 2:
                out[...] = block
            else:
                out[half] = block


def back(d, own, other):
    planes, rows, width = d.shape
    g, _, _, r, e = own.shape
    tile = 4
    spec = pl.BlockSpec((tile, 2, planes, r, e), lambda t: (t, 0, 0, 0, 0))
    half = g * r
    pair = jax.ShapeDtypeStruct((2, 128, half), BF16)
    single = jax.ShapeDtypeStruct((128, half), BF16)
    pair_spec = pl.BlockSpec((2, 128, tile * r), lambda t: (0, 0, t))
    single_spec = pl.BlockSpec((128, tile * r), lambda t: (0, t))
    return pl.pallas_call(
        back_kernel,
        out_shape=[pair, pair, single, single, pair],
        grid=(g // tile,),
        in_specs=[pl.BlockSpec((planes, rows, width), lambda t: (0, 0, 0)), spec, spec],
        out_specs=[pair_spec, pair_spec, single_spec, single_spec, pair_spec],
        compiler_params=params(),
        cost_estimate=cost(4 * rows * half * width * planes, 2 * (d.size + 2 * own.size + 2 * rows * half)),
    )(d, own, other)


def weight_kernel(x_ref, d_ref, *refs):
    out_ref, xt = refs[-2:]
    @pl.when(pl.program_id(0) == 0)
    def _():
        xt[...] = x_ref[0].T

    total = jnp.dot(xt[...], d_ref[0], preferred_element_type=F32)
    g, _, _, r, e = out_ref.shape
    for s in range(2):
        part = total[:, s * e : (s + 1) * e].reshape(g, r, e)
        if len(refs) == 3:
            part = part + refs[0][:, s, 0].astype(F32)
        out_ref[:, s, 0] = part.astype(BF16)


def weight_grad(x, side, d, received=None):
    planes, rows, width = d.shape
    half = x.shape[2]
    g, e = 8, width // 2
    r = half // g
    spec = pl.BlockSpec((g, 2, 1, r, e), lambda p: (0, 0, p, 0, 0))
    more = [] if received is None else [received]
    return pl.pallas_call(
        weight_kernel,
        out_shape=jax.ShapeDtypeStruct((g, 2, planes, r, e), BF16),
        grid=(planes,),
        in_specs=[
            pl.BlockSpec((1, rows, half), lambda p: (side, 0, 0)),
            pl.BlockSpec((1, rows, width), lambda p: (p, 0, 0)),
        ]
        + [spec] * len(more),
        out_specs=spec,
        scratch_shapes=[pltpu.VMEM((half, rows), BF16)],
        compiler_params=params(),
        cost_estimate=cost(2 * rows * half * width * planes, 2 * (half * width * planes * 2 + d.size)),
    )(x, d, *more)


def scatter_z(y0, y1, y2a, y2b, y3):
    ra, rb = hop(y2a, 1), hop(y2b, 3)
    y3 = jnp.stack([(y3[0].astype(F32) + ra.astype(F32)).astype(BF16), y3[1]])
    y1 = jnp.stack([y1[0], (y1[1].astype(F32) + rb.astype(F32)).astype(BF16)])
    r3, r1 = hop(y3, 3), hop(y1, 1)
    return y0.astype(F32) + r1.astype(F32) + r3.astype(F32)


def per_device(inputs, w_qkv, w_out, upstream):
    core = lax.axis_index("c")
    r, _, e = w_qkv.shape
    gather = lambda w: lax.all_gather(w, XY, axis=0, tiled=False).reshape(8, 2, -1, r, e)
    qkv_own = gather(w_qkv.transpose(1, 0, 2))
    out_own = gather(w_out.T[None])

    inputs_float = inputs.astype(F32)
    centred = inputs_float - jnp.mean(inputs_float, axis=1, keepdims=True)
    inv_scale = lax.rsqrt(jnp.mean(centred * centred, axis=1, keepdims=True) + EPS)
    standard = centred * inv_scale
    n0 = halves(standard.astype(BF16), core)
    u0 = halves(upstream, core)
    n1, n3 = hop(n0, 1), hop(n0, 3)
    n2 = hop(n3, 1)
    u1, u3 = hop(u0, 1), hop(u0, 3)
    u2 = hop(u1, 3)
    normed = jnp.concatenate([n0, n1, n2, n3], axis=1)
    cotangent = jnp.concatenate([u0, u1, u2, u3], axis=1)

    qkv_other = swap(qkv_own)
    out_other = swap(out_own)
    projected = project(normed, qkv_own, qkv_other)
    grad_context = project(cotangent, out_own, out_other)[0]
    context, grad_projected = attention(projected, grad_context)

    context1 = context[None]
    g_out = weight_grad(cotangent, 1, context1)
    g_qkv = weight_grad(normed, 1, grad_projected)
    g_out = weight_grad(cotangent, 0, context1, swap(g_out))
    g_qkv = weight_grad(normed, 0, grad_projected, swap(g_qkv))
    scatter = lambda v: lax.psum_scatter(
        v.reshape(16, -1, r, e), XY, scatter_dimension=0, tiled=False
    )
    grad_wout = scatter(g_out)[0].T
    grad_wqkv = scatter(g_qkv).transpose(1, 0, 2)

    attended = whole(scatter_z(*back(context1, out_own, out_other)), core)
    layer_out = (inputs_float + attended).astype(BF16)

    grad_normed = whole(scatter_z(*back(grad_projected, qkv_own, qkv_other)), core)
    centre_grad = jnp.mean(grad_normed, axis=1, keepdims=True)
    along = jnp.mean(grad_normed * standard, axis=1, keepdims=True)
    grad_x = (
        upstream.astype(F32) + inv_scale * (grad_normed - centre_grad - standard * along)
    ).astype(BF16)
    return layer_out, grad_x, grad_wqkv, grad_wout


def solution(mesh):
    fine = Mesh(mesh.devices.reshape(4, 2, 2, 2, 4), ALL)
    dp, mp = ("y", "xh", "c"), ("xl", "z")
    rows = P(ALL, None)
    return jax.shard_map(
        per_device,
        mesh=fine,
        in_specs=(rows, P(dp, None, mp), P(mp, dp), rows),
        out_specs=(rows, rows, P(dp, None, mp), P(mp, dp)),
        check_vma=False,
    )
```

```python
import jax
import jax.numpy as jnp
from jax import lax
from jax.experimental import pallas as pl
from jax.experimental.pallas import tpu as pltpu
from jax.sharding import Mesh, PartitionSpec as P

HD = 128
PATCH = 256
ROWS = 128
EPS = 1e-06
F32 = jnp.float32
BF16 = jnp.bfloat16
XY = ("y", "xh", "xl")
ALL = ("y", "xh", "c", "xl", "z")
NT = (((1,), (1,)), ((), ()))
TN = (((0,), (0,)), ((), ()))


def call(kernel, out, grid, in_specs, out_specs, scratch=(), flops=0, nbytes=0):
    return pl.pallas_call(
        kernel,
        out_shape=out,
        grid=grid,
        in_specs=in_specs,
        out_specs=out_specs,
        scratch_shapes=scratch,
        compiler_params=pltpu.CompilerParams(vmem_limit_bytes=56 * 1024 * 1024),
        cost_estimate=pl.CostEstimate(flops=int(flops), bytes_accessed=int(nbytes), transcendentals=0),
    )


def array(shape, dtype=BF16):
    return jax.ShapeDtypeStruct(shape, dtype)


def full(*shape):
    return pl.BlockSpec(shape, lambda t: (0,) * len(shape))


def hop(value, distance):
    return lax.ppermute(value, "z", [(i, i ^ distance) for i in range(4)])


def swap(value):
    return lax.ppermute(value, "c", [(0, 1), (1, 0)])


def low_lanes(width):
    return lax.broadcasted_iota(jnp.int32, (ROWS, width), 1) < width // 2


def split_columns(values, core):
    pair = values.shape[1] // 8
    low = low_lanes(pair)
    mine, theirs = [], []
    for s in range(0, 8, 2):
        first, second = values[:, s * pair : (s + 1) * pair], values[:, (s + 1) * pair : (s + 2) * pair]
        even = jnp.where(low, first, pltpu.roll(second, pair // 2, 1))
        odd = jnp.where(low, pltpu.roll(first, pair // 2, 1), second)
        mine.append(jnp.where(core == 0, even, odd))
        theirs.append(jnp.where(core == 0, odd, even))
    return jnp.concatenate(mine, axis=1), jnp.concatenate(theirs, axis=1)


def join_columns(mine, theirs, core):
    pair = mine.shape[1] // 4
    low = low_lanes(pair)
    out = []
    for s in range(4):
        a, b = mine[:, s * pair : (s + 1) * pair], theirs[:, s * pair : (s + 1) * pair]
        even, odd = jnp.where(core == 0, a, b), jnp.where(core == 0, b, a)
        out.append(jnp.where(low, even, pltpu.roll(odd, pair // 2, 1)))
        out.append(jnp.where(low, pltpu.roll(even, pair // 2, 1), odd))
    return jnp.concatenate(out, axis=1)


def standardize(values):
    values = values.astype(F32)
    centred = values - jnp.mean(values, axis=1, keepdims=True)
    inv = lax.rsqrt(jnp.mean(centred * centred, axis=1, keepdims=True) + EPS)
    return centred * inv, inv


def prepare_kernel(core_ref, x_ref, u_ref, mine_n, mine_u, send):
    core = core_ref[0]
    standard, _ = standardize(x_ref[...])
    for t, (values, mine) in enumerate(((standard, mine_n), (u_ref[...].astype(F32), mine_u))):
        a, b = split_columns(values, core)
        mine[...] = a.astype(BF16)
        send[t] = b.astype(BF16)


def prepare(core, inputs, upstream):
    rows, width = inputs.shape
    half = width // 2
    return call(
        prepare_kernel,
        [array((rows, half)), array((rows, half)), array((2, rows, half))],
        (1,),
        [pl.BlockSpec(memory_space=pltpu.SMEM), full(rows, width), full(rows, width)],
        [full(rows, half), full(rows, half), full(2, rows, half)],
        nbytes=8 * rows * width,
    )(core, inputs, upstream)


def transpose_kernel(*refs):
    *blocks, n_out, u_out = refs
    for out, group in ((n_out, blocks[:4]), (u_out, blocks[4:])):
        for k in range(2):
            for j in range(4):
                at = (k * 4 + j) * ROWS
                out[:, at : at + ROWS] = group[j][k].T


def transpose(n, u):
    half = n[0].shape[2]
    return call(
        transpose_kernel,
        [array((half, 8 * ROWS))] * 2,
        (1,),
        [full(2, ROWS, half)] * 8,
        [full(half, 8 * ROWS)] * 2,
        nbytes=64 * ROWS * half,
    )(*n, *u)


def both(ref, plane=0):
    g, _, _, r, e = ref.shape
    return jnp.concatenate(
        [ref[:, 0, plane].reshape(g * r, e), ref[:, 1, plane].reshape(g * r, e)], axis=1
    )


def project_kernel(side, kinds, received, refs):
    count = len(set(kinds))
    w_ref, out_ref = refs[4 * count], refs[-1]
    for kind in sorted(set(kinds)):
        steps = [p for p, k in enumerate(kinds) if k == kind]

        @pl.when((pl.program_id(0) >= steps[0]) & (pl.program_id(0) <= steps[-1]))
        def _(kind=kind):
            blocks = refs[4 * kind : 4 * kind + 4]
            x = jnp.concatenate([b[side] for b in blocks], axis=0)
            total = jnp.dot(x, both(w_ref), preferred_element_type=F32)
            if received:
                total = total + refs[-2][0]
            out_ref[0] = total.astype(out_ref.dtype)


def project(side, kinds, first, blocks, weights, received=None):
    g, _, _, r, e = weights.shape
    half = g * r
    flat = [b for group in blocks for b in group]
    out = pl.BlockSpec((1, 4 * ROWS, 2 * e), lambda p: (p, 0, 0))
    more = [] if received is None else [received]

    def kernel(*refs):
        project_kernel(side, kinds, bool(more), refs)

    return call(
        kernel,
        array((len(kinds), 4 * ROWS, 2 * e), BF16 if more else F32),
        (len(kinds),),
        [full(2, ROWS, half)] * len(flat)
        + [pl.BlockSpec((g, 2, 1, r, e), lambda p: (0, 0, p + first, 0, 0))]
        + [out] * len(more),
        out,
        flops=2 * 4 * ROWS * half * 2 * e * len(kinds),
        nbytes=(half * 2 * e * 2 + 4 * ROWS * 2 * e * 6) * len(kinds),
    )(*flat, weights, *more)


def attention_kernel(a_ref, b_ref, d_ref):
    scale = HD ** (-0.5)
    for h in range(a_ref.shape[2] // HD):
        cols = slice(h * HD, (h + 1) * HD)
        q, k, v, g = a_ref[0, :, cols], a_ref[1, :, cols], b_ref[0, :, cols], b_ref[1, :, cols]
        scores = lax.dot_general(q, k, NT, preferred_element_type=F32) * scale
        weights = jnp.exp(scores - jnp.max(scores, axis=1, keepdims=True))
        probs = weights / jnp.sum(weights, axis=1, keepdims=True)
        probs16 = probs.astype(BF16)
        d_ref[3, :, cols] = jnp.dot(probs16, v, preferred_element_type=F32).astype(BF16)
        gp = lax.dot_general(g, v, NT, preferred_element_type=F32)
        d_ref[2, :, cols] = lax.dot_general(probs16, g, TN, preferred_element_type=F32).astype(BF16)
        totals = jnp.sum(probs * gp, axis=1, keepdims=True)
        gs = (probs * (gp - totals) * scale).astype(BF16)
        d_ref[0, :, cols] = jnp.dot(gs, k, preferred_element_type=F32).astype(BF16)
        d_ref[1, :, cols] = lax.dot_general(gs, q, TN, preferred_element_type=F32).astype(BF16)


def attention(part, qk, vg):
    _, rows, width = qk.shape
    cols = width // 2
    spec = pl.BlockSpec((2, PATCH, cols), lambda i: (0, i, part))
    return call(
        attention_kernel,
        array((4, rows, cols)),
        (rows // PATCH,),
        [spec, spec],
        pl.BlockSpec((4, PATCH, cols), lambda i: (0, i, 0)),
        flops=14 * rows * PATCH * cols * 2,
        nbytes=16 * rows * cols,
    )(qk, vg)


def weight_kernel(nt_ref, ut_ref, m0, m1, t0, t1, out_ref):
    d = jnp.concatenate(
        [jnp.concatenate([m0[0], m1[0]], axis=1), jnp.concatenate([t0[0], t1[0]], axis=1)], axis=0
    )
    g, _, _, r, e = out_ref.shape

    def emit(x_ref):
        total = jnp.dot(x_ref[...], d, preferred_element_type=F32).astype(BF16)
        for s in range(2):
            out_ref[:, s, 0] = total[:, s * e : (s + 1) * e].reshape(g, r, e)

    pl.when(pl.program_id(0) < 3)(lambda: emit(nt_ref))
    pl.when(pl.program_id(0) == 3)(lambda: emit(ut_ref))


def weight_grads(nt, ut, mine, theirs):
    half, tokens = nt.shape
    planes, rows, e = mine[0].shape
    r = half // 8
    spec = pl.BlockSpec((1, rows, e), lambda p: (p, 0, 0))
    return call(
        weight_kernel,
        array((8, 2, planes, r, e)),
        (planes,),
        [full(half, tokens)] * 2 + [spec] * 4,
        pl.BlockSpec((8, 2, 1, r, e), lambda p: (0, 0, p, 0, 0)),
        flops=2 * half * tokens * 2 * e * planes,
        nbytes=2 * (2 * half * tokens + half * 2 * e * planes + tokens * 2 * e * planes),
    )(nt, ut, *mine, *theirs)


def back_kernel(m0, m1, t0, t1, w_ref, y0, y1, y2a, y2b, y3):
    planes = w_ref.shape[2]
    for side, (left, right) in enumerate(((m0, m1), (t0, t1))):
        total = None
        for p in range(planes):
            d = jnp.concatenate([left[p], right[p]], axis=1)
            term = lax.dot_general(d, both(w_ref, p), NT, preferred_element_type=F32)
            total = term if total is None else total + term
        total = total.astype(BF16)
        for j, out in enumerate((y0, y1, (y2a, y2b)[side], y3)):
            block = total[j * ROWS : (j + 1) * ROWS]
            if j == 2:
                out[...] = block
            else:
                out[side] = block


def back(first, planes, mine, theirs, weights):
    g, _, _, r, e = weights.shape
    tile = 4
    rows = mine[0].shape[1]
    half = g * r
    d_spec = pl.BlockSpec((planes, rows, e), lambda t: (first // planes, 0, 0))
    pair_spec = pl.BlockSpec((2, ROWS, tile * r), lambda t: (0, 0, t))
    single_spec = pl.BlockSpec((ROWS, tile * r), lambda t: (0, t))
    pair, single = array((2, ROWS, half)), array((ROWS, half))
    return call(
        back_kernel,
        [pair, pair, single, single, pair],
        (g // tile,),
        [d_spec] * 4
        + [pl.BlockSpec((tile, 2, planes, r, e), lambda t: (t, 0, first // planes, 0, 0))],
        [pair_spec, pair_spec, single_spec, single_spec, pair_spec],
        flops=2 * 2 * rows * half * 2 * e * planes,
        nbytes=2 * (half * 2 * e * planes + 4 * rows * e * planes + 2 * rows * half),
    )(*mine, *theirs, weights)


def scatter_z(y0, y1, y2a, y2b, y3):
    add = lambda a, b: (a.astype(F32) + b.astype(F32)).astype(BF16)
    ra, rb = hop(y2a, 1), hop(y2b, 3)
    y3 = jnp.stack([add(y3[0], ra), y3[1]])
    y1 = jnp.stack([y1[0], add(y1[1], rb)])
    r3, r1 = hop(y3, 3), hop(y1, 1)
    total = [y0[k].astype(F32) + r1[k].astype(F32) + r3[k].astype(F32) for k in range(2)]
    return total[0], swap(total[1])


def layer_out_kernel(core_ref, x_ref, mine, theirs, out_ref):
    out_ref[...] = (
        x_ref[...].astype(F32) + join_columns(mine[...], theirs[...], core_ref[0])
    ).astype(BF16)


def grad_x_kernel(core_ref, x_ref, u_ref, mine, theirs, out_ref):
    grad = join_columns(mine[...], theirs[...], core_ref[0])
    standard, inv = standardize(x_ref[...])
    centre = jnp.mean(grad, axis=1, keepdims=True)
    along = jnp.mean(grad * standard, axis=1, keepdims=True)
    out_ref[...] = (u_ref[...].astype(F32) + inv * (grad - centre - standard * along)).astype(BF16)


def finish(kernel, core, arrays, mine, theirs):
    rows, width = arrays[0].shape
    return call(
        kernel,
        array((rows, width)),
        (1,),
        [pl.BlockSpec(memory_space=pltpu.SMEM)]
        + [full(rows, width)] * len(arrays)
        + [full(rows, width // 2)] * 2,
        full(rows, width),
        nbytes=12 * rows * width,
    )(core, *arrays, mine, theirs)


def per_device(inputs, w_qkv, w_out, upstream):
    core = lax.axis_index("c").astype(jnp.int32).reshape(1)
    r, _, e = w_qkv.shape
    planes = jnp.concatenate([w_qkv.transpose(1, 0, 2), w_out.T[None]])
    weights = lax.all_gather(planes, XY, axis=0, tiled=False).reshape(8, 2, 4, r, e)

    mine_n, mine_u, send = prepare(core, inputs, upstream)
    got = swap(send)
    n0, u0 = jnp.stack([mine_n, got[0]]), jnp.stack([mine_u, got[1]])
    n1, n3 = hop(n0, 1), hop(n0, 3)
    n2 = hop(n3, 1)
    u1, u3 = hop(u0, 1), hop(u0, 3)
    u2 = hop(u1, 3)
    n, u = (n0, n1, n2, n3), (u0, u1, u2, u3)
    nt, ut = transpose(n, u)

    qk_sent = swap(project(1, (0, 0), 0, (n,), weights))
    vg_sent = swap(project(1, (0, 1), 2, (n, u), weights))
    qk = project(0, (0, 0), 0, (n,), weights, qk_sent)
    vg = project(0, (0, 1), 2, (n, u), weights, vg_sent)
    mine = [attention(part, qk, vg) for part in range(2)]
    theirs = [swap(d) for d in mine]

    grads = weight_grads(nt, ut, mine, theirs)
    grads = lax.psum_scatter(grads.reshape(64 * r, e), XY, scatter_dimension=0, tiled=True)
    grads = grads.reshape(4, r, e)
    grad_wqkv = grads[:3].transpose(1, 0, 2)
    grad_wout = grads[3].T

    layer_out = finish(
        layer_out_kernel, core, (inputs,), *scatter_z(*back(3, 1, mine, theirs, weights))
    )
    grad_x = finish(
        grad_x_kernel, core, (inputs, upstream), *scatter_z(*back(0, 3, mine, theirs, weights))
    )
    return layer_out, grad_x, grad_wqkv, grad_wout


def solution(mesh):
    fine = Mesh(mesh.devices.reshape(4, 2, 2, 2, 4), ALL)
    dp, mp = ("y", "xh", "c"), ("xl", "z")
    rows = P(ALL, None)
    return jax.shard_map(
        per_device,
        mesh=fine,
        in_specs=(rows, P(dp, None, mp), P(mp, dp), rows),
        out_specs=(rows, rows, P(dp, None, mp), P(mp, dp)),
        check_vma=False,
    )
```

```python
import jax
import jax.numpy as jnp
from jax import lax
from jax.experimental import pallas as pl
from jax.experimental.pallas import tpu as pltpu
from jax.sharding import Mesh, PartitionSpec as P

HD = 128
PATCH = 256
ROWS = 128
EPS = 1e-06
F32 = jnp.float32
BF16 = jnp.bfloat16
XY = ("y", "xh", "xl")
X_AXIS = ("xh", "xl")
ALL = ("y", "xh", "c", "xl", "z")
NT = (((1,), (1,)), ((), ()))
TN = (((0,), (0,)), ((), ()))


def call(kernel, out, grid, in_specs, out_specs, scratch=(), flops=0, nbytes=0):
    return pl.pallas_call(
        kernel,
        out_shape=out,
        grid=grid,
        in_specs=in_specs,
        out_specs=out_specs,
        scratch_shapes=scratch,
        compiler_params=pltpu.CompilerParams(vmem_limit_bytes=34 * 1024 * 1024),
        cost_estimate=pl.CostEstimate(flops=int(flops), bytes_accessed=int(nbytes), transcendentals=0),
    )


def array(shape, dtype=BF16):
    return jax.ShapeDtypeStruct(shape, dtype)


def full(*shape):
    return pl.BlockSpec(shape, lambda t: (0,) * len(shape))


def along(axis, value, distance):
    return lax.ppermute(value, axis, [(i, i ^ distance) for i in range(4)])


def swap(value):
    return lax.ppermute(value, "c", [(0, 1), (1, 0)])


def low_lanes(width):
    return lax.broadcasted_iota(jnp.int32, (ROWS, width), 1) < width // 2


def split_columns(values, core):
    pair = values.shape[1] // 8
    low = low_lanes(pair)
    mine, theirs = [], []
    for s in range(0, 8, 2):
        first, second = values[:, s * pair : (s + 1) * pair], values[:, (s + 1) * pair : (s + 2) * pair]
        even = jnp.where(low, first, pltpu.roll(second, pair // 2, 1))
        odd = jnp.where(low, pltpu.roll(first, pair // 2, 1), second)
        mine.append(jnp.where(core == 0, even, odd))
        theirs.append(jnp.where(core == 0, odd, even))
    return jnp.concatenate(mine, axis=1), jnp.concatenate(theirs, axis=1)


def join_columns(mine, theirs, core):
    pair = mine.shape[1] // 4
    low = low_lanes(pair)
    out = []
    for s in range(4):
        a, b = mine[:, s * pair : (s + 1) * pair], theirs[:, s * pair : (s + 1) * pair]
        even, odd = jnp.where(core == 0, a, b), jnp.where(core == 0, b, a)
        out.append(jnp.where(low, even, pltpu.roll(odd, pair // 2, 1)))
        out.append(jnp.where(low, pltpu.roll(even, pair // 2, 1), odd))
    return jnp.concatenate(out, axis=1)


def standardize(values):
    values = values.astype(F32)
    centred = values - jnp.mean(values, axis=1, keepdims=True)
    inv = lax.rsqrt(jnp.mean(centred * centred, axis=1, keepdims=True) + EPS)
    return centred * inv, inv


def prepare_kernel(core_ref, x_ref, u_ref, mine_n, mine_u, send):
    core = core_ref[0]
    standard, _ = standardize(x_ref[...])
    for t, (values, mine) in enumerate(((standard, mine_n), (u_ref[...].astype(F32), mine_u))):
        a, b = split_columns(values, core)
        mine[...] = a.astype(BF16)
        send[t] = b.astype(BF16)


def prepare(core, inputs, upstream):
    rows, width = inputs.shape
    half = width // 2
    return call(
        prepare_kernel,
        [array((rows, half)), array((rows, half)), array((2, rows, half))],
        (1,),
        [pl.BlockSpec(memory_space=pltpu.SMEM), full(rows, width), full(rows, width)],
        [full(rows, half), full(rows, half), full(2, rows, half)],
        nbytes=8 * rows * width,
    )(core, inputs, upstream)


def transpose_kernel(*refs):
    *blocks, n_out, u_out = refs
    for out, group in ((n_out, blocks[:4]), (u_out, blocks[4:])):
        for k in range(2):
            for j in range(4):
                at = (k * 4 + j) * ROWS
                out[:, at : at + ROWS] = group[j][k].T


def transpose(n, u):
    half = n[0].shape[2]
    return call(
        transpose_kernel,
        [array((half, 8 * ROWS))] * 2,
        (1,),
        [full(2, ROWS, half)] * 8,
        [full(half, 8 * ROWS)] * 2,
        nbytes=64 * ROWS * half,
    )(*n, *u)


def both(ref, plane=0):
    g, _, _, r, e = ref.shape
    return jnp.concatenate(
        [ref[:, 0, plane].reshape(g * r, e), ref[:, 1, plane].reshape(g * r, e)], axis=1
    )


def project(n, u, weights):
    g, _, planes, r, e = weights.shape
    half = g * r

    def kernel(n0, n1, u0, u1, w_ref, mine, sent):
        def emit(blocks):
            x = jnp.concatenate([b[side] for side in range(2) for b in blocks], axis=0)
            total = jnp.dot(x, both(w_ref), preferred_element_type=F32)
            mine[0] = total[:PATCH]
            sent[0] = total[PATCH:]

        pl.when(pl.program_id(0) < planes - 1)(lambda: emit((n0, n1)))
        pl.when(pl.program_id(0) == planes - 1)(lambda: emit((u0, u1)))

    return call(
        kernel,
        [array((planes, PATCH, 2 * e), F32)] * 2,
        (planes,),
        [full(2, ROWS, half)] * 4 + [pl.BlockSpec((g, 2, 1, r, e), lambda p: (0, 0, p, 0, 0))],
        [pl.BlockSpec((1, PATCH, 2 * e), lambda p: (p, 0, 0))] * 2,
        flops=4 * PATCH * half * 2 * e * planes,
        nbytes=(half * 2 * e * 2 + 2 * PATCH * 2 * e * 4) * planes,
    )(*n, *u, weights)


def attention_kernel(mine, got, d_ref):
    scale = HD ** (-0.5)
    for h in range(d_ref.shape[2] // HD):
        cols = slice(h * HD, (h + 1) * HD)
        q, k, v, g = [(mine[i, :, cols] + got[i, :, cols]).astype(BF16) for i in range(4)]
        scores = lax.dot_general(q, k, NT, preferred_element_type=F32) * scale
        weights = jnp.exp(scores - jnp.max(scores, axis=1, keepdims=True))
        probs = weights / jnp.sum(weights, axis=1, keepdims=True)
        probs16 = probs.astype(BF16)
        d_ref[3, :, cols] = jnp.dot(probs16, v, preferred_element_type=F32).astype(BF16)
        gp = lax.dot_general(g, v, NT, preferred_element_type=F32)
        d_ref[2, :, cols] = lax.dot_general(probs16, g, TN, preferred_element_type=F32).astype(BF16)
        totals = jnp.sum(probs * gp, axis=1, keepdims=True)
        gs = (probs * (gp - totals) * scale).astype(BF16)
        d_ref[0, :, cols] = jnp.dot(gs, k, preferred_element_type=F32).astype(BF16)
        d_ref[1, :, cols] = lax.dot_general(gs, q, TN, preferred_element_type=F32).astype(BF16)


def attention(mine, got):
    planes, rows, width = mine.shape
    spec = pl.BlockSpec((planes, rows, width // 2), lambda h: (0, 0, h))
    return call(
        attention_kernel,
        array((planes, rows, width)),
        (2,),
        [spec] * 2,
        spec,
        flops=14 * rows * PATCH * width * 2,
        nbytes=40 * rows * width,
    )(mine, got)


def weight_kernel(nt_ref, ut_ref, m0, m1, t0, t1, out_ref):
    d = jnp.concatenate([m0[0], m1[0], t0[0], t1[0]], axis=0)
    g, _, _, r, e = out_ref.shape

    def emit(x_ref):
        total = jnp.dot(x_ref[...], d, preferred_element_type=F32).astype(BF16)
        for s in range(2):
            out_ref[:, s, 0] = total[:, s * e : (s + 1) * e].reshape(g, r, e)

    pl.when(pl.program_id(0) < 3)(lambda: emit(nt_ref))
    pl.when(pl.program_id(0) == 3)(lambda: emit(ut_ref))


def weight_grads(nt, ut, mine, theirs):
    half, tokens = nt.shape
    planes, rows, width = mine[0].shape
    r, e = half // 8, width // 2
    spec = pl.BlockSpec((1, rows, width), lambda p: (p, 0, 0))
    return call(
        weight_kernel,
        array((8, 2, planes, r, e)),
        (planes,),
        [full(half, tokens)] * 2 + [spec] * 4,
        pl.BlockSpec((8, 2, 1, r, e), lambda p: (0, 0, p, 0, 0)),
        flops=2 * half * tokens * width * planes,
        nbytes=2 * (2 * half * tokens + half * width * planes + tokens * width * planes),
    )(nt, ut, *mine, *theirs)


def back_kernel(m0, m1, t0, t1, w_ref, y0, y1, y2a, y2b, y3):
    planes = w_ref.shape[2]
    for side, (first, second) in enumerate(((m0, m1), (t0, t1))):
        total = None
        for p in range(planes):
            d = jnp.concatenate([first[p], second[p]], axis=0)
            term = lax.dot_general(d, both(w_ref, p), NT, preferred_element_type=F32)
            total = term if total is None else total + term
        total = total.astype(BF16)
        for j, out in enumerate((y0, y1, (y2a, y2b)[side], y3)):
            block = total[j * ROWS : (j + 1) * ROWS]
            if j == 2:
                out[...] = block
            else:
                out[side] = block


def back(first, planes, mine, theirs, weights):
    g, _, _, r, e = weights.shape
    tile = 4
    half = g * r
    rows, width = mine[0].shape[1:]
    d_spec = pl.BlockSpec((planes, rows, width), lambda t: (first // planes, 0, 0))
    pair_spec = pl.BlockSpec((2, ROWS, tile * r), lambda t: (0, 0, t))
    single_spec = pl.BlockSpec((ROWS, tile * r), lambda t: (0, t))
    pair, single = array((2, ROWS, half)), array((ROWS, half))
    return call(
        back_kernel,
        [pair, pair, single, single, pair],
        (g // tile,),
        [d_spec] * 4
        + [pl.BlockSpec((tile, 2, planes, r, e), lambda t: (t, 0, first // planes, 0, 0))],
        [pair_spec, pair_spec, single_spec, single_spec, pair_spec],
        flops=8 * rows * half * width * planes,
        nbytes=2 * (half * width * planes + 4 * rows * width * planes + 4 * rows * half),
    )(*mine, *theirs, weights)


def scatter_z(y0, y1, y2a, y2b, y3):
    add = lambda a, b: (a.astype(F32) + b.astype(F32)).astype(BF16)
    ra, rb = along("z", y2a, 1), along("z", y2b, 3)
    y3 = jnp.stack([add(y3[0], ra), y3[1]])
    y1 = jnp.stack([y1[0], add(y1[1], rb)])
    r3, r1 = along("z", y3, 3), along("z", y1, 1)
    total = [y0[k].astype(F32) + r1[k].astype(F32) + r3[k].astype(F32) for k in range(2)]
    return total[0], swap(total[1])


def part_kernel(in_ref, qkv, wout):
    qkv[...] = in_ref[:3]
    wout[...] = in_ref[3]


def part_planes(grads):
    planes, r, e = grads.shape
    return call(
        part_kernel,
        [array((3, r, e)), array((r, e))],
        (1,),
        [full(planes, r, e)],
        [full(3, r, e), full(r, e)],
        nbytes=4 * grads.size,
    )(grads)


def layer_out_kernel(core_ref, x_ref, mine, theirs, out_ref):
    out_ref[...] = (
        x_ref[...].astype(F32) + join_columns(mine[...], theirs[...], core_ref[0])
    ).astype(BF16)


def grad_x_kernel(core_ref, x_ref, u_ref, mine, theirs, out_ref):
    grad = join_columns(mine[...], theirs[...], core_ref[0])
    standard, inv = standardize(x_ref[...])
    centre = jnp.mean(grad, axis=1, keepdims=True)
    along = jnp.mean(grad * standard, axis=1, keepdims=True)
    out_ref[...] = (u_ref[...].astype(F32) + inv * (grad - centre - standard * along)).astype(BF16)


def finish(kernel, core, arrays, mine, theirs):
    rows, width = arrays[0].shape
    return call(
        kernel,
        array((rows, width)),
        (1,),
        [pl.BlockSpec(memory_space=pltpu.SMEM)]
        + [full(rows, width)] * len(arrays)
        + [full(rows, width // 2)] * 2,
        full(rows, width),
        nbytes=12 * rows * width,
    )(core, *arrays, mine, theirs)


def per_device(inputs, w_qkv, w_out, upstream):
    core = lax.axis_index("c").astype(jnp.int32).reshape(1)
    r, _, e = w_qkv.shape
    planes = jnp.concatenate([w_qkv.transpose(1, 0, 2), w_out.T[None]])
    weights = lax.all_gather(planes, XY, axis=0, tiled=False).reshape(8, 2, 4, r, e)

    mine_n, mine_u, send = prepare(core, inputs, upstream)
    got = swap(send)
    n0, u0 = jnp.stack([mine_n, got[0]]), jnp.stack([mine_u, got[1]])
    n1, n3 = along("z", n0, 1), along("z", n0, 3)
    n2 = along("z", n3, 1)
    u1, u3 = along("z", u0, 1), along("z", u0, 3)
    u2 = along("z", u1, 3)
    n, u = (n0, n1, n2, n3), (u0, u1, u2, u3)
    nt, ut = transpose(n, u)
    weights, nt, ut = lax.optimization_barrier((weights, nt, ut))

    mine = []
    for image in range(2):
        at = slice(2 * image, 2 * image + 2)
        own, sent = project(n[at], u[at], weights)
        mine.append((own, swap(sent)))
    mine = [attention(own, got) for own, got in mine]
    theirs = [swap(d) for d in mine]

    grads = weight_grads(nt, ut, mine, theirs)
    grads = lax.psum_scatter(grads.reshape(64 * r, e), XY, scatter_dimension=0, tiled=True)
    grad_wqkv, grad_wout = part_planes(grads.reshape(4, r, e))
    grad_wqkv, grad_wout = grad_wqkv.transpose(1, 0, 2), grad_wout.T

    attended = back(3, 1, mine, theirs, weights)
    layer_out = finish(layer_out_kernel, core, (inputs,), *scatter_z(*attended))
    grad_normed = back(0, 3, mine, theirs, weights)
    grad_x = finish(grad_x_kernel, core, (inputs, upstream), *scatter_z(*grad_normed))
    return layer_out, grad_x, grad_wqkv, grad_wout


def solution(mesh):
    fine = Mesh(mesh.devices.reshape(4, 2, 2, 2, 4), ALL)
    dp, mp = ("y", "xh", "c"), ("xl", "z")
    rows = P(ALL, None)
    return jax.shard_map(
        per_device,
        mesh=fine,
        in_specs=(rows, P(dp, None, mp), P(mp, dp), rows),
        out_specs=(rows, rows, P(dp, None, mp), P(mp, dp)),
        check_vma=False,
    )
```
